1024 devices in a mesh: ctx: 128 (over y, z_hi, x, core), tp: 8 (over z_lo).
Axes of the slice: x: 4, y: 8, z: 16 (z_hi: 2, z_lo: 8; z = z_hi * 8 + z_lo), core: 2. Of those that a mesh axis runs over, the one named last changes fastest.
Arguments:
- residual: bfloat16 [32768, 4096], P('ctx', 'tp'), may hold values from -6 to 6
- proj: bfloat16 [32768, 3, 4096], P('ctx', None, 'tp'), may hold values from -5 to 5
- short_filter: bfloat16 [7, 3, 4096], P(None, None, 'tp'), may hold values from -2.5 to 2.5
- medium_filter: bfloat16 [128, 4096], P(None, 'tp'), may hold values from -4 to 4
- skip: float32 [4096], P('tp'), may hold values from -3 to 3
- out_weight: bfloat16 [4096, 4096], P('ctx', 'tp'), may hold values from -0.09375 to 0.09375
Outputs:
- block_out: bfloat16 [32768, 4096], P('ctx', 'tp')
The draws below stay inside these ranges and needn't reach their ends.
All inputs are finite; a program needn't handle non-finite values.
Results may differ from the reference program's by a relative error of at most 0.0085.
Values may be sent and summed in bfloat16 or wider, within the bound.
No kernel may reach another device: no remote copies, remote signals or barrier semaphores. Data moves between devices by JAX's collectives and lax.ppermute only.
A program may use at most 64 MiB of HBM per device.

```python
import jax
import jax.numpy as jnp
from jax import lax

D = 4096
SHORT = 7
MEDIUM = 128
TOKENS = 32768


def draw_medium_filter(key, part):
    first, second = jax.random.split(jax.random.fold_in(key, 11))
    lower, upper = (0.25, 6.0)
    spans = jnp.exp(jax.random.uniform(first, (1, D), jnp.float32, jnp.log(lower), jnp.log(upper)))
    decay = spans / MEDIUM
    lags = jnp.arange(MEDIUM, dtype=jnp.float32)[:, None]
    scale = jnp.sqrt(2.0 * decay / (1.0 - jnp.exp(-2.0 * spans)))
    values = jax.random.truncated_normal(second, -3.0, 3.0, (MEDIUM, D), jnp.float32)
    return (values * jnp.exp(-decay * lags) * scale).astype(jnp.bfloat16)


def block_scale(stream_key, extent, shards, low, largest):
    loudness = 1.0
    for axis_at, parts in shards:
        heights = jax.random.uniform(jax.random.fold_in(jax.random.fold_in(stream_key, 6), axis_at), (parts,), jnp.float32, low / len(shards), largest / len(shards))
        loudness = loudness * jnp.repeat(jnp.exp(heights), extent[axis_at] // parts).reshape((-1,) + (1,) * (len(extent) - 1 - axis_at))
    return loudness


def bell_draw(own_key, extent, scale, limit, pieces=(), kind=jnp.bfloat16):
    result = scale * jax.random.normal(own_key, extent, jnp.float32)
    if pieces:
        result = result * block_scale(own_key, extent, pieces, -0.22, 0.18)
    return jnp.clip(result, -limit, limit).astype(kind)


def setup_inputs(seed: int = 0) -> dict:
    streams_of = jax.random.split(jax.random.key(seed), 7)
    residual = bell_draw(streams_of[0], (TOKENS, D), 1.0, 6.0, ((0, 128), (1, 8)))
    proj = bell_draw(streams_of[1], (TOKENS, 3, D), 1.0, 5.0, ((0, 128), (2, 8)))
    short_filter = bell_draw(streams_of[2], (SHORT, 3, D), 0.4, 2.5, ((2, 8),))
    medium_filter = draw_medium_filter(jax.random.fold_in(streams_of[6], 71), 0)
    skip = bell_draw(streams_of[4], (D,), 1.0, 3.0, ((0, 8),), jnp.float32)
    out_weight = bell_draw(streams_of[5], (D, D), D ** -0.5, 0.09375, ((0, 128), (1, 8)))
    return {"residual": residual, "proj": proj, "short_filter": short_filter, "medium_filter": medium_filter, "skip": skip, "out_weight": out_weight}


def channel_block(args):
    streams, short_f, medium_f, skip_b = args
    tokens = streams.shape[0]
    taps = short_f.shape[0]
    padded = jnp.concatenate([jnp.zeros((taps - 1,) + streams.shape[1:], jnp.float32), streams.astype(jnp.float32)], 0)
    mixed = jnp.zeros(streams.shape, jnp.float32)
    for j in range(taps):
        mixed = mixed + short_f[j].astype(jnp.float32) * padded[taps - 1 - j: taps - 1 - j + tokens]
    product = (mixed[:, 1] * mixed[:, 2]).astype(jnp.bfloat16)
    length = 2 * tokens
    spectrum = jnp.fft.rfft(product.astype(jnp.float32), n=length, axis=0) * jnp.fft.rfft(medium_f.astype(jnp.float32), n=length, axis=0)
    filtered = jnp.fft.irfft(spectrum, n=length, axis=0)[:tokens]
    filtered = filtered + skip_b * product.astype(jnp.float32)
    return (mixed[:, 0] * filtered).astype(jnp.bfloat16)


def reference(residual, proj, short_filter, medium_filter, skip, out_weight):
    width = 256
    groups = D // width
    streams = jnp.moveaxis(proj.reshape(TOKENS, 3, groups, width), 2, 0)
    short_g = jnp.moveaxis(short_filter.reshape(SHORT, 3, groups, width), 2, 0)
    medium_g = jnp.moveaxis(medium_filter.reshape(MEDIUM, groups, width), 1, 0)
    skip_g = skip.reshape(groups, width)
    gated = lax.map(channel_block, (streams, short_g, medium_g, skip_g))
    gated = jnp.moveaxis(gated, 0, 1).reshape(TOKENS, D)
    total = jnp.dot(gated, out_weight, preferred_element_type=jnp.float32)
    return (residual.astype(jnp.float32) + total).astype(jnp.bfloat16)
```

```python
import functools

import jax
import jax.numpy as jnp
import numpy as np
from jax import lax
from jax.experimental import pallas as pl
from jax.experimental.pallas import tpu as pltpu
from jax.sharding import Mesh, PartitionSpec as P


SPAN = 256
HALF = 128
HEAD = 144
TAIL = 16
WROWS = 32
PACK = 256

F32 = jnp.float32
BF16 = jnp.bfloat16


def split(matrix):
    high = matrix.astype(np.float32).astype(BF16)
    low = (matrix - high.astype(np.float64)).astype(np.float32).astype(BF16)
    return high, low


def dft_matrices():
    n = np.arange(SPAN)
    k = np.arange(HALF)[:, None]
    angle = 2.0 * np.pi * ((k * n) % SPAN) / SPAN
    cos, sin = np.cos(angle), np.sin(angle)
    nyquist = np.where(n % 2 == 0, 1.0, -1.0)
    forward = np.concatenate([cos, -sin], 0)
    forward[HALF] = nyquist
    inverse = np.concatenate([2.0 * cos, -2.0 * sin], 0)
    inverse[0] = 1.0
    inverse[HALF] = nyquist
    inverse = inverse.T[HALF:] / SPAN
    fh, fl = split(forward)
    ih, il = split(inverse)
    return np.concatenate([fh, fl], 0), np.concatenate([ih, ih, il], 1)


def dot(a, b):
    return jnp.dot(a, b, preferred_element_type=F32)


def spectrum(forward, values):
    both = dot(forward, values)
    return both[:SPAN] + both[SPAN:]


def times(x, f):
    xr, xi, fr, fi = x[:HALF], x[HALF:], f[:HALF], f[HALF:]
    real = lax.broadcasted_iota(jnp.int32, xr.shape, 0) == 0
    rr, ii = xr * fr, xi * fi
    out_r = jnp.where(real, rr, rr - ii)
    out_i = jnp.where(real, ii, xr * fi + xi * fr)
    y = jnp.concatenate([out_r, out_i], 0)
    high = y.astype(BF16)
    low = (y - high.astype(F32)).astype(BF16)
    return jnp.concatenate([high, low, high], 0)


def taps(ext, filt, start, count):
    total = None
    for j in range(filt.shape[0]):
        term = filt[j : j + 1] * ext[pl.ds(start - j, count), :]
        total = term if total is None else total + term
    return total


def local_kernel(p, sf, w, pack, prod, q, ext):
    rows = p.shape[1]
    step = 64
    filt = sf[...].astype(F32)
    ext[...] = jnp.zeros_like(ext)
    for c in range(3):
        ext[c, pl.ds(8, rows), :] = p[c].astype(F32)
    for r in reversed(range(0, rows, step)):
        mixed = [taps(ext.at[c], filt[c], 8 + r, step) for c in range(3)]
        q[pl.ds(r, step), :] = mixed[0]
        prod[pl.ds(r, step), :] = (mixed[1] * mixed[2]).astype(BF16)
    pack[pl.ds(0, WROWS), :] = w[...]
    pack[pl.ds(WROWS, HALF), :] = prod[pl.ds(rows - HALF, HALF), :]
    for c in range(3):
        pack[pl.ds(WROWS + HALF + c * TAIL, TAIL), :] = p[c, pl.ds(rows - TAIL, TAIL), :]
    used = WROWS + HALF + 3 * TAIL
    pack[pl.ds(used, PACK - used), :] = jnp.zeros((PACK - used, p.shape[2]), BF16)


def late_kernel(prod, q, mf, skip, fwd, inv, out, spec):
    f = spectrum(fwd[:, pl.ds(0, HALF)], mf[...])
    spec[...] = f
    y = times(spectrum(fwd[...], prod[...]), f)
    skipped = HEAD - HALF
    rows = prod.shape[0] - HEAD
    filtered = dot(inv[pl.ds(skipped, rows), :], y)
    filtered = filtered + skip[...] * prod[pl.ds(HEAD, rows), :].astype(F32)
    out[...] = (q[pl.ds(HEAD, rows), :] * filtered).astype(BF16)


def early_kernel(p, halo, sf, prod, q, spec, skip, fwd, inv, out, ext, win):
    filt = sf[...].astype(F32)
    mixed = []
    for c in range(3):
        ext[c, pl.ds(0, TAIL), :] = halo[pl.ds(HALF + c * TAIL, TAIL), :].astype(F32)
        ext[c, pl.ds(TAIL, TAIL), :] = p[c, pl.ds(0, TAIL), :].astype(F32)
        mixed.append(taps(ext.at[c], filt[c], TAIL, TAIL))
    win[pl.ds(0, HALF), :] = halo[pl.ds(0, HALF), :]
    win[pl.ds(HALF, TAIL), :] = (mixed[1] * mixed[2]).astype(BF16)
    win[pl.ds(HALF + TAIL, SPAN - TAIL), :] = prod[pl.ds(TAIL, SPAN - TAIL), :]
    f = spec[...]
    first = dot(inv[...], times(spectrum(fwd[...], win[pl.ds(0, SPAN), :]), f))
    second = times(spectrum(fwd[...], win[pl.ds(HALF, SPAN), :]), f)
    second = dot(inv[pl.ds(0, HEAD - HALF), :], second)
    cur = win[pl.ds(HALF, HEAD), :].astype(F32) * skip[...]
    out[pl.ds(0, TAIL), :] = (mixed[0] * (first[:TAIL] + cur[:TAIL])).astype(BF16)
    mid = HALF - TAIL
    out[pl.ds(TAIL, mid), :] = (
        q[pl.ds(TAIL, mid), :] * (first[TAIL:] + cur[TAIL:HALF])
    ).astype(BF16)
    rest = HEAD - HALF
    out[pl.ds(HALF, rest), :] = (q[pl.ds(HALF, rest), :] * (second + cur[HALF:])).astype(BF16)


def final_kernel(place, *refs):
    early, late = refs[:15], refs[15:30]
    residual, w, out, wv, sem = refs[30:]
    me, x = place[0], place[1]
    blocks = wv.shape[0]
    copies = []
    for s in range(blocks):
        owner = lax.rem(me - s + blocks, blocks)
        own = []
        for core in range(2):
            for rel in range(4):
                at = lax.rem(x + rel, 4)
                own.append(
                    pltpu.make_async_copy(
                        w.at[owner, core, rel], wv.at[s, :, at, core], sem.at[s, core * 4 + rel]
                    )
                )
        for copy in own:
            copy.start()
        copies.append(own)
    total_e = total_l = None
    for s in range(blocks):
        for copy in copies[s]:
            copy.wait()
        block = wv[s].reshape(512, 512)

        def piece(group):
            if s == 0:
                return group[0][...]
            return jnp.where(me >= s, group[s][...], group[15 - s][...])

        add_e, add_l = dot(piece(early), block), dot(piece(late), block)
        total_e = add_e if total_e is None else total_e + add_e
        total_l = add_l if total_l is None else total_l + add_l
    rows = early[0].shape[0]
    out[pl.ds(0, rows), :] = (residual[pl.ds(0, rows), :].astype(F32) + total_e).astype(BF16)
    rest = late[0].shape[0]
    out[pl.ds(rows, rest), :] = (residual[pl.ds(rows, rest), :].astype(F32) + total_l).astype(BF16)


def sds(shape, dtype):
    return jax.ShapeDtypeStruct(shape, dtype)


def cost(flops, nbytes):
    return pl.CostEstimate(flops=flops, bytes_accessed=nbytes, transcendentals=0)


def along_line(own):
    up = [(i, i + 1) for i in range(7)]
    down = [(i + 1, i) for i in range(7)]
    right, left, rights, lefts = own, own, [], []
    for _ in range(7):
        right = lax.ppermute(right, "tp", up)
        left = lax.ppermute(left, "tp", down)
        rights.append(right)
        lefts.append(left)
    return [own] + rights + lefts


def on_device(residual, proj, short_filter, medium_filter, skip, out_weight):
    rows, chans = residual.shape
    fwd, inv = (jnp.asarray(m) for m in dft_matrices())
    p = jnp.transpose(proj, (1, 0, 2))
    sf = jnp.transpose(short_filter, (1, 0, 2))
    skip = skip.reshape(1, chans)
    x, zh, core, me = (lax.axis_index(a) for a in ("x", "zh", "core", "tp"))

    pack, prod, q = pl.pallas_call(
        local_kernel,
        out_shape=(sds((PACK, chans), BF16), sds((rows, chans), BF16), sds((rows, chans), F32)),
        scratch_shapes=[pltpu.VMEM((3, rows + 8, chans), F32)],
        cost_estimate=cost(6_000_000, 2_000_000),
        name="local",
    )(p, sf, out_weight)

    both = lax.all_gather(pack, "zh", axis=0)

    late, spec = pl.pallas_call(
        late_kernel,
        out_shape=(sds((rows - HEAD, chans), BF16), sds((SPAN, chans), F32)),
        cost_estimate=cost(300_000_000, 3_000_000),
        name="late",
    )(prod, q, medium_filter, skip, fwd, inv)

    ends = (x == 3) & (core == 1)
    which = jnp.where(ends, 1 - zh, zh)
    tail = lax.dynamic_slice(
        both, (which, WROWS, 0), (1, HALF + 3 * TAIL, chans)
    ).reshape(HALF + 3 * TAIL, chans)
    pairs = []
    for yy in range(8):
        for zz in range(2):
            base = (yy * 2 + zz) * 8
            pairs += [(base + i, base + i + 1) for i in range(7)]
            if zz == 1:
                pairs.append((base + 7, base))
            elif yy < 7:
                pairs.append((base + 7, base + 16))
    halo = lax.ppermute(tail, ("y", "zh", "x", "core"), pairs)

    mine = both[:, :WROWS, :]
    nxt = lax.ppermute(mine, "x", [((i + 1) % 4, i) for i in range(4)])
    opp = lax.ppermute(mine, "x", [((i + 2) % 4, i) for i in range(4)])
    prv = lax.ppermute(mine, "x", [((i + 3) % 4, i) for i in range(4)])
    row = jnp.stack([mine, nxt, opp, prv])
    weight = lax.all_gather(row, ("y", "core"), axis=0)
    weight = weight.reshape(8, 2, 4, 2, WROWS, chans)

    late_parts = along_line(late)

    early = pl.pallas_call(
        early_kernel,
        out_shape=sds((HEAD, chans), BF16),
        scratch_shapes=[
            pltpu.VMEM((3, 2 * TAIL, chans), F32),
            pltpu.VMEM((HALF + SPAN, chans), BF16),
        ],
        cost_estimate=cost(600_000_000, 3_000_000),
        name="early",
    )(p, halo, sf, prod, q, spec, skip, fwd, inv)
    early_parts = along_line(early)

    place = jnp.stack([me, x]).astype(jnp.int32)
    vmem = pl.BlockSpec(memory_space=pltpu.VMEM)
    return pl.pallas_call(
        final_kernel,
        out_shape=sds((rows, chans), BF16),
        in_specs=[pl.BlockSpec(memory_space=pltpu.SMEM)]
        + [vmem] * 31
        + [pl.BlockSpec(memory_space=pl.ANY)],
        out_specs=vmem,
        scratch_shapes=[
            pltpu.VMEM((8, 2, 4, 2, WROWS, chans), BF16),
            pltpu.SemaphoreType.DMA((8, 8)),
        ],
        cost_estimate=cost(2 * rows * 8 * chans * chans, 8_000_000),
        name="project",
    )(place, *early_parts, *late_parts, residual, weight)


def solution(mesh):
    devices = np.asarray(mesh.devices).reshape(8, 2, 4, 2, 8)
    fine = Mesh(devices, ("y", "zh", "x", "core", "tp"))
    ctx = ("y", "zh", "x", "core")
    in_specs = (
        P(ctx, "tp"),
        P(ctx, None, "tp"),
        P(None, None, "tp"),
        P(None, "tp"),
        P("tp"),
        P(ctx, "tp"),
    )
    return jax.shard_map(
        on_device, mesh=fine, in_specs=in_specs, out_specs=P(ctx, "tp"), check_vma=False
    )
```

```python
import jax
import jax.numpy as jnp
import numpy as np
from jax import lax
from jax.experimental import pallas as pl
from jax.experimental.pallas import tpu as pltpu
from jax.sharding import Mesh, PartitionSpec as P


SPAN = 256
HALF = 128
HEAD = 144
TAIL = 16
WROWS = 32
PACK = WROWS + HALF + 3 * TAIL

F32 = jnp.float32
BF16 = jnp.bfloat16


def split(matrix):
    high = matrix.astype(np.float32).astype(BF16)
    low = (matrix - high.astype(np.float64)).astype(np.float32).astype(BF16)
    return high, low


def dft_matrices():
    n = np.arange(SPAN)
    k = np.arange(HALF)[:, None]
    angle = 2.0 * np.pi * ((k * n) % SPAN) / SPAN
    cos, sin = np.cos(angle), np.sin(angle)
    nyquist = np.where(n % 2 == 0, 1.0, -1.0)
    forward = np.concatenate([cos, -sin], 0)
    forward[HALF] = nyquist
    inverse = np.concatenate([2.0 * cos, -2.0 * sin], 0)
    inverse[0] = 1.0
    inverse[HALF] = nyquist
    inverse = inverse.T[HALF:] / SPAN
    fh, fl = split(forward)
    ih, il = split(inverse)
    return np.concatenate([fh, fl], 0), np.concatenate([ih, ih, il], 1)


def dot(a, b):
    return jnp.dot(a, b, preferred_element_type=F32)


def spectrum(forward, values):
    both = dot(forward, values)
    return both[:SPAN] + both[SPAN:]


def times(x, f):
    xr, xi, fr, fi = x[:HALF], x[HALF:], f[:HALF], f[HALF:]
    real = lax.broadcasted_iota(jnp.int32, xr.shape, 0) == 0
    rr, ii = xr * fr, xi * fi
    out_r = jnp.where(real, rr, rr - ii)
    out_i = jnp.where(real, ii, xr * fi + xi * fr)
    y = jnp.concatenate([out_r, out_i], 0)
    high = y.astype(BF16)
    low = (y - high.astype(F32)).astype(BF16)
    return jnp.concatenate([high, low, high], 0)


def taps(ext, filt, start, count):
    total = None
    for j in range(filt.shape[0]):
        term = filt[j : j + 1] * ext[pl.ds(start - j, count), :]
        total = term if total is None else total + term
    return total


def local_kernel(p, sf, w, pack, prod, q, ext):
    rows = p.shape[1]
    step = 64
    filt = sf[...].astype(F32)
    ext[...] = jnp.zeros_like(ext)
    for c in range(3):
        ext[c, pl.ds(8, rows), :] = p[c].astype(F32)
    for r in reversed(range(0, rows, step)):
        mixed = [taps(ext.at[c], filt[c], 8 + r, step) for c in range(3)]
        q[pl.ds(r, step), :] = mixed[0]
        prod[pl.ds(r, step), :] = (mixed[1] * mixed[2]).astype(BF16)
    pack[pl.ds(0, WROWS), :] = w[...]
    pack[pl.ds(WROWS, HALF), :] = prod[pl.ds(rows - HALF, HALF), :]
    for c in range(3):
        pack[pl.ds(WROWS + HALF + c * TAIL, TAIL), :] = p[c, pl.ds(rows - TAIL, TAIL), :]


def late_kernel(prod, q, mf, skip, fwd, inv, out, spec):
    f = spectrum(fwd[:, pl.ds(0, HALF)], mf[...])
    spec[...] = f
    y = times(spectrum(fwd[...], prod[...]), f)
    skipped = HEAD - HALF
    rows = prod.shape[0] - HEAD
    filtered = dot(inv[pl.ds(skipped, rows), :], y)
    filtered = filtered + skip[...] * prod[pl.ds(HEAD, rows), :].astype(F32)
    out[...] = (q[pl.ds(HEAD, rows), :] * filtered).astype(BF16)


def early_kernel(p, halo, sf, prod, q, late, spec, skip, fwd, inv, out, ext, win):
    filt = sf[...].astype(F32)
    mixed = []
    for c in range(3):
        ext[c, pl.ds(0, TAIL), :] = halo[pl.ds(HALF + c * TAIL, TAIL), :].astype(F32)
        ext[c, pl.ds(TAIL, TAIL), :] = p[c, pl.ds(0, TAIL), :].astype(F32)
        mixed.append(taps(ext.at[c], filt[c], TAIL, TAIL))
    win[pl.ds(0, HALF), :] = halo[pl.ds(0, HALF), :]
    win[pl.ds(HALF, TAIL), :] = (mixed[1] * mixed[2]).astype(BF16)
    win[pl.ds(HALF + TAIL, SPAN - TAIL), :] = prod[pl.ds(TAIL, SPAN - TAIL), :]
    f = spec[...]
    first = dot(inv[...], times(spectrum(fwd[...], win[pl.ds(0, SPAN), :]), f))
    second = times(spectrum(fwd[...], win[pl.ds(HALF, SPAN), :]), f)
    second = dot(inv[pl.ds(0, HEAD - HALF), :], second)
    cur = win[pl.ds(HALF, HEAD), :].astype(F32) * skip[...]
    out[pl.ds(0, TAIL), :] = (mixed[0] * (first[:TAIL] + cur[:TAIL])).astype(BF16)
    mid = HALF - TAIL
    out[pl.ds(TAIL, mid), :] = (
        q[pl.ds(TAIL, mid), :] * (first[TAIL:] + cur[TAIL:HALF])
    ).astype(BF16)
    rest = HEAD - HALF
    out[pl.ds(HALF, rest), :] = (q[pl.ds(HALF, rest), :] * (second + cur[HALF:])).astype(BF16)
    out[pl.ds(HEAD, late.shape[0]), :] = late[...]


def final_kernel(place, *refs):
    parts = refs[:8]
    residual, w, out, wv, sem = refs[8:]
    me, x, zh = place[0], place[1], place[2]
    blocks = wv.shape[0]
    copies = []
    for s in range(blocks):
        owner = lax.bitwise_xor(me, s)
        own = []
        for core in range(2):
            for rel in range(4):
                for other in range(2):
                    source = w.at[owner, core, rel, other]
                    target = wv.at[s, lax.rem(zh + other, 2), lax.rem(x + rel, 4), core]
                    own.append(
                        pltpu.make_async_copy(source, target, sem.at[s, core * 8 + rel * 2 + other])
                    )
        for copy in own:
            copy.start()
        copies.append(own)
    total = residual[...].astype(F32)
    for s in range(blocks):
        for copy in copies[s]:
            copy.wait()
        total = total + dot(parts[s][...], wv[s].reshape(512, 512))
    out[...] = total.astype(BF16)


def sds(shape, dtype):
    return jax.ShapeDtypeStruct(shape, dtype)


def cost(flops, nbytes):
    return pl.CostEstimate(flops=flops, bytes_accessed=nbytes, transcendentals=0)


def across_line(own):
    def swap(piece, by):
        return lax.ppermute(piece, "tp", [(i, i ^ by) for i in range(8)])

    four, two, one = swap(own, 4), swap(own, 2), swap(own, 1)
    six, five, three = swap(four, 2), swap(four, 1), swap(two, 1)
    return [own, one, two, three, four, five, six, swap(six, 1)]


def on_device(residual, proj, short_filter, medium_filter, skip, out_weight):
    rows, chans = residual.shape
    fwd, inv = (jnp.asarray(m) for m in dft_matrices())
    p = jnp.transpose(proj, (1, 0, 2))
    sf = jnp.transpose(short_filter, (1, 0, 2))
    skip = skip.reshape(1, chans)
    x, zh, core, me = (lax.axis_index(a) for a in ("x", "zh", "core", "tp"))

    pack, prod, q = pl.pallas_call(
        local_kernel,
        out_shape=(sds((PACK, chans), BF16), sds((rows, chans), BF16), sds((rows, chans), F32)),
        scratch_shapes=[pltpu.VMEM((3, rows + 8, chans), F32)],
        cost_estimate=cost(6_000_000, 2_000_000),
        name="local",
    )(p, sf, out_weight)

    over = lax.ppermute(pack, "zh", [(0, 1), (1, 0)])

    late, spec = pl.pallas_call(
        late_kernel,
        out_shape=(sds((rows - HEAD, chans), BF16), sds((SPAN, chans), F32)),
        cost_estimate=cost(300_000_000, 3_000_000),
        name="late",
    )(prod, q, medium_filter, skip, fwd, inv)

    over, late = lax.optimization_barrier((over, late))

    ends = (x == 3) & (core == 1)
    tail = jnp.where(ends, over[WROWS:], pack[WROWS:])
    pairs = []
    for yy in range(8):
        for zz in range(2):
            base = (yy * 2 + zz) * 8
            pairs += [(base + i, base + i + 1) for i in range(7)]
            if zz == 1:
                pairs.append((base + 7, base))
            elif yy < 7:
                pairs.append((base + 7, base + 16))
    halo = lax.ppermute(tail, ("y", "zh", "x", "core"), pairs)

    mine = jnp.stack([out_weight, over[:WROWS]])
    nxt = lax.ppermute(mine, "x", [((i + 1) % 4, i) for i in range(4)])
    opp = lax.ppermute(mine, "x", [((i + 2) % 4, i) for i in range(4)])
    prv = lax.ppermute(mine, "x", [((i + 3) % 4, i) for i in range(4)])
    nxt, opp, prv, halo = lax.optimization_barrier((nxt, opp, prv, halo))
    row = jnp.stack([mine, nxt, opp, prv])
    weight = lax.all_gather(row, ("y", "core"), axis=0)
    weight = weight.reshape(8, 2, 4, 2, WROWS, chans)

    gated = pl.pallas_call(
        early_kernel,
        out_shape=sds((rows, chans), BF16),
        scratch_shapes=[
            pltpu.VMEM((3, 2 * TAIL, chans), F32),
            pltpu.VMEM((HALF + SPAN, chans), BF16),
        ],
        cost_estimate=cost(600_000_000, 3_000_000),
        name="early",
    )(p, halo, sf, prod, q, late, spec, skip, fwd, inv)
    parts = across_line(gated)

    place = jnp.stack([me, x, zh]).astype(jnp.int32)
    vmem = pl.BlockSpec(memory_space=pltpu.VMEM)
    return pl.pallas_call(
        final_kernel,
        out_shape=sds((rows, chans), BF16),
        in_specs=[pl.BlockSpec(memory_space=pltpu.SMEM)]
        + [vmem] * 9
        + [pl.BlockSpec(memory_space=pl.ANY)],
        out_specs=vmem,
        scratch_shapes=[
            pltpu.VMEM((8, 2, 4, 2, WROWS, chans), BF16),
            pltpu.SemaphoreType.DMA((8, 16)),
        ],
        cost_estimate=cost(2 * rows * 8 * chans * chans, 8_000_000),
        name="project",
    )(place, *parts, residual, weight)


def solution(mesh):
    devices = np.asarray(mesh.devices).reshape(8, 2, 4, 2, 8)
    fine = Mesh(devices, ("y", "zh", "x", "core", "tp"))
    ctx = ("y", "zh", "x", "core")
    in_specs = (
        P(ctx, "tp"),
        P(ctx, None, "tp"),
        P(None, None, "tp"),
        P(None, "tp"),
        P("tp"),
        P(ctx, "tp"),
    )
    return jax.shard_map(
        on_device, mesh=fine, in_specs=in_specs, out_specs=P(ctx, "tp"), check_vma=False
    )
```

```python
import jax
import jax.numpy as jnp
import numpy as np
from jax import lax
from jax.experimental import pallas as pl
from jax.experimental.pallas import tpu as pltpu
from jax.sharding import Mesh, PartitionSpec as P


SPAN = 256
HALF = 128
HEAD = 144
TAIL = 16
WROWS = 32
PACK = HALF + 3 * TAIL

F32 = jnp.float32
BF16 = jnp.bfloat16


def split(matrix):
    high = matrix.astype(np.float32).astype(BF16)
    low = (matrix - high.astype(np.float64)).astype(np.float32).astype(BF16)
    return high, low


def dft_matrices():
    n = np.arange(SPAN)
    k = np.arange(HALF)[:, None]
    angle = 2.0 * np.pi * ((k * n) % SPAN) / SPAN
    cos, sin = np.cos(angle), np.sin(angle)
    nyquist = np.where(n % 2 == 0, 1.0, -1.0)
    forward = np.concatenate([cos, -sin], 0)
    forward[HALF] = nyquist
    inverse = np.concatenate([2.0 * cos, -2.0 * sin], 0)
    inverse[0] = 1.0
    inverse[HALF] = nyquist
    inverse = inverse.T[HALF:] / SPAN
    fh, fl = split(forward)
    ih, il = split(inverse)
    return np.concatenate([fh, fl], 0), np.concatenate([ih, ih, il], 1)


def dot(a, b):
    return jnp.dot(a, b, preferred_element_type=F32)


def spectrum(forward, values):
    both = dot(forward, values)
    return both[:SPAN] + both[SPAN:]


def times(x, f):
    xr, xi, fr, fi = x[:HALF], x[HALF:], f[:HALF], f[HALF:]
    real = lax.broadcasted_iota(jnp.int32, xr.shape, 0) == 0
    rr, ii = xr * fr, xi * fi
    out_r = jnp.where(real, rr, rr - ii)
    out_i = jnp.where(real, ii, xr * fi + xi * fr)
    y = jnp.concatenate([out_r, out_i], 0)
    high = y.astype(BF16)
    low = (y - high.astype(F32)).astype(BF16)
    return jnp.concatenate([high, low, high], 0)


def taps(ext, filt, start, count):
    total = None
    for j in range(filt.shape[0]):
        term = filt[j : j + 1] * ext[pl.ds(start - j, count), :]
        total = term if total is None else total + term
    return total


def local_kernel(p, sf, pack, prod, q, ext):
    rows = p.shape[1]
    step = 64
    filt = sf[...].astype(F32)
    ext[...] = jnp.zeros_like(ext)
    for c in range(3):
        ext[c, pl.ds(8, rows), :] = p[c].astype(F32)
    for r in reversed(range(0, rows, step)):
        mixed = [taps(ext.at[c], filt[c], 8 + r, step) for c in range(3)]
        q[pl.ds(r, step), :] = mixed[0]
        prod[pl.ds(r, step), :] = (mixed[1] * mixed[2]).astype(BF16)
    pack[pl.ds(0, HALF), :] = prod[pl.ds(rows - HALF, HALF), :]
    for c in range(3):
        pack[pl.ds(HALF + c * TAIL, TAIL), :] = p[c, pl.ds(rows - TAIL, TAIL), :]


def late_kernel(prod, q, mf, skip, fwd, inv, out, spec):
    f = spectrum(fwd[:, pl.ds(0, HALF)], mf[...])
    spec[...] = f
    y = times(spectrum(fwd[...], prod[...]), f)
    skipped = HEAD - HALF
    rows = prod.shape[0] - HEAD
    filtered = dot(inv[pl.ds(skipped, rows), :], y)
    filtered = filtered + skip[...] * prod[pl.ds(HEAD, rows), :].astype(F32)
    out[...] = (q[pl.ds(HEAD, rows), :] * filtered).astype(BF16)


def early_kernel(p, halo, sf, prod, q, late, spec, skip, fwd, inv, out, ext, win):
    filt = sf[...].astype(F32)
    mixed = []
    for c in range(3):
        ext[c, pl.ds(0, TAIL), :] = halo[pl.ds(HALF + c * TAIL, TAIL), :].astype(F32)
        ext[c, pl.ds(TAIL, TAIL), :] = p[c, pl.ds(0, TAIL), :].astype(F32)
        mixed.append(taps(ext.at[c], filt[c], TAIL, TAIL))
    win[pl.ds(0, HALF), :] = halo[pl.ds(0, HALF), :]
    win[pl.ds(HALF, TAIL), :] = (mixed[1] * mixed[2]).astype(BF16)
    win[pl.ds(HALF + TAIL, SPAN - TAIL), :] = prod[pl.ds(TAIL, SPAN - TAIL), :]
    f = spec[...]
    first = dot(inv[...], times(spectrum(fwd[...], win[pl.ds(0, SPAN), :]), f))
    second = times(spectrum(fwd[...], win[pl.ds(HALF, SPAN), :]), f)
    second = dot(inv[pl.ds(0, HEAD - HALF), :], second)
    cur = win[pl.ds(HALF, HEAD), :].astype(F32) * skip[...]
    mid = HALF - TAIL
    rest = HEAD - HALF
    pieces = [
        (0, TAIL, mixed[0] * (first[:TAIL] + cur[:TAIL])),
        (TAIL, mid, q[pl.ds(TAIL, mid), :] * (first[TAIL:] + cur[TAIL:HALF])),
        (HALF, rest, q[pl.ds(HALF, rest), :] * (second + cur[HALF:])),
        (HEAD, late.shape[0], late[...]),
    ]
    for at, count, value in pieces:
        value = value.astype(BF16)
        for i in range(out.shape[0]):
            out[i, pl.ds(at, count), :] = value


def final_kernel(place, near, far, residual, *refs):
    weights, (out, wv, sem) = refs[:8], refs[8:]
    half, zh, y = place[0], place[1], place[2]
    copies = []
    for i, weight in enumerate(weights):
        for other in range(2):
            target = wv.at[lax.rem(y + i, 8), lax.rem(zh + other, 2)]
            copies.append(pltpu.make_async_copy(weight.at[:, other], target, sem.at[i, other]))
    for copy in copies:
        copy.start()
    total = residual[...].astype(F32)
    for copy in copies:
        copy.wait()
    for s in range(8):
        owner = 4 * (half if s < 4 else 1 - half) + s % 4
        part = near[s] if s < 4 else far[s - 4]
        total = total + dot(part, wv[owner].reshape(512, 512))
    out[...] = total.astype(BF16)


def sds(shape, dtype):
    return jax.ShapeDtypeStruct(shape, dtype)


def cost(flops, nbytes):
    return pl.CostEstimate(flops=flops, bytes_accessed=nbytes, transcendentals=0)


def to_all(copies, axis):
    return lax.all_to_all(copies, axis, 0, 0)


def around_y(own):
    up, down, ups, downs = own, own, [], []
    for step in range(4):
        up = lax.ppermute(up, "y", [(i, (i + 1) % 8) for i in range(8)])
        ups.append(up)
        if step < 3:
            down = lax.ppermute(down, "y", [((i + 1) % 8, i) for i in range(8)])
            downs.append(down)
    return [own] + downs + ups[::-1]


def on_device(residual, proj, short_filter, medium_filter, skip, out_weight):
    rows, chans = residual.shape
    fwd, inv = (jnp.asarray(m) for m in dft_matrices())
    p = jnp.transpose(proj, (1, 0, 2))
    sf = jnp.transpose(short_filter, (1, 0, 2))
    skip = skip.reshape(1, chans)
    half, zh, y = (lax.axis_index(a) for a in ("half", "zh", "y"))

    over = lax.ppermute(out_weight, "zh", [(0, 1), (1, 0)])

    pack, prod, q = pl.pallas_call(
        local_kernel,
        out_shape=(sds((PACK, chans), BF16), sds((rows, chans), BF16), sds((rows, chans), F32)),
        scratch_shapes=[pltpu.VMEM((3, rows + 8, chans), F32)],
        cost_estimate=cost(6_000_000, 2_000_000),
        name="local",
    )(p, sf)

    halo = lax.ppermute(pack, ("y", "zh", "x", "core"), [(i, i + 1) for i in range(127)])

    late, spec = pl.pallas_call(
        late_kernel,
        out_shape=(sds((rows - HEAD, chans), BF16), sds((SPAN, chans), F32)),
        cost_estimate=cost(300_000_000, 3_000_000),
        name="late",
    )(prod, q, medium_filter, skip, fwd, inv)

    over, late = lax.optimization_barrier((over, late))

    mine = jnp.broadcast_to(jnp.stack([out_weight, over]), (8, 2, WROWS, chans))
    row = to_all(mine, ("x", "core"))

    gated = pl.pallas_call(
        early_kernel,
        out_shape=sds((4, rows, chans), BF16),
        scratch_shapes=[
            pltpu.VMEM((3, 2 * TAIL, chans), F32),
            pltpu.VMEM((HALF + SPAN, chans), BF16),
        ],
        cost_estimate=cost(600_000_000, 3_000_000),
        name="early",
    )(p, halo, sf, prod, q, late, spec, skip, fwd, inv)
    gated, row = lax.optimization_barrier((gated, row))

    weights = around_y(row)

    across = lax.ppermute(gated[0], "half", [(0, 1), (1, 0)])
    near = to_all(gated, "quarter")
    far = to_all(jnp.broadcast_to(across, (4, rows, chans)), "quarter")

    place = jnp.stack([half, zh, y]).astype(jnp.int32)
    vmem = pl.BlockSpec(memory_space=pltpu.VMEM)
    return pl.pallas_call(
        final_kernel,
        out_shape=sds((rows, chans), BF16),
        in_specs=[pl.BlockSpec(memory_space=pltpu.SMEM)]
        + [vmem] * 3
        + [pl.BlockSpec(memory_space=pl.ANY)] * 8,
        out_specs=vmem,
        scratch_shapes=[
            pltpu.VMEM((8, 2, 8, WROWS, chans), BF16),
            pltpu.SemaphoreType.DMA((8, 2)),
        ],
        cost_estimate=cost(2 * rows * 8 * chans * chans, 8_000_000),
        name="project",
    )(place, near, far, residual, *weights)


def solution(mesh):
    devices = np.asarray(mesh.devices).reshape(8, 2, 4, 2, 2, 4)
    fine = Mesh(devices, ("y", "zh", "x", "core", "half", "quarter"))
    ctx = ("y", "zh", "x", "core")
    tp = ("half", "quarter")
    in_specs = (
        P(ctx, tp),
        P(ctx, None, tp),
        P(None, None, tp),
        P(None, tp),
        P(tp),
        P(ctx, tp),
    )

    return jax.shard_map(
        on_device, mesh=fine, in_specs=in_specs, out_specs=P(ctx, tp), check_vma=False
    )
```

```python
import jax
import jax.numpy as jnp
import numpy as np
from jax import lax
from jax.experimental import pallas as pl
from jax.experimental.pallas import tpu as pltpu
from jax.sharding import Mesh, PartitionSpec as P


SPAN = 256
HALF = 128
HEAD = 144
TAIL = 16
WROWS = 32
PACK = HALF + 3 * TAIL

F32 = jnp.float32
BF16 = jnp.bfloat16


def split(matrix):
    high = matrix.astype(np.float32).astype(BF16)
    low = (matrix - high.astype(np.float64)).astype(np.float32).astype(BF16)
    return high, low


def dft_matrices():
    n = np.arange(SPAN)
    k = np.arange(HALF)[:, None]
    angle = 2.0 * np.pi * ((k * n) % SPAN) / SPAN
    cos, sin = np.cos(angle), np.sin(angle)
    nyquist = np.where(n % 2 == 0, 1.0, -1.0)
    forward = np.concatenate([cos, -sin], 0)
    forward[HALF] = nyquist
    inverse = np.concatenate([2.0 * cos, -2.0 * sin], 0)
    inverse[0] = 1.0
    inverse[HALF] = nyquist
    inverse = inverse.T[HALF:] / SPAN
    fh, fl = split(forward)
    ih, il = split(inverse)
    return np.concatenate([fh, fl], 0), np.concatenate([ih, ih, il], 1)


def dot(a, b):
    return jnp.dot(a, b, preferred_element_type=F32)


def spectrum(forward, values):
    both = dot(forward, values)
    return both[:SPAN] + both[SPAN:]


def times(x, f):
    xr, xi, fr, fi = x[:HALF], x[HALF:], f[:HALF], f[HALF:]
    real = lax.broadcasted_iota(jnp.int32, xr.shape, 0) == 0
    rr, ii = xr * fr, xi * fi
    out_r = jnp.where(real, rr, rr - ii)
    out_i = jnp.where(real, ii, xr * fi + xi * fr)
    y = jnp.concatenate([out_r, out_i], 0)
    high = y.astype(BF16)
    low = (y - high.astype(F32)).astype(BF16)
    return jnp.concatenate([high, low, high], 0)


def taps(ext, filt, start, count):
    total = None
    for j in range(filt.shape[0]):
        term = filt[j : j + 1] * ext[pl.ds(start - j, count), :]
        total = term if total is None else total + term
    return total


def local_kernel(p, sf, pack, prod, q, ext):
    rows = p.shape[1]
    step = 64
    filt = sf[...].astype(F32)
    ext[...] = jnp.zeros_like(ext)
    for c in range(3):
        ext[c, pl.ds(8, rows), :] = p[c].astype(F32)
    for r in reversed(range(0, rows, step)):
        mixed = [taps(ext.at[c], filt[c], 8 + r, step) for c in range(3)]
        q[pl.ds(r, step), :] = mixed[0]
        prod[pl.ds(r, step), :] = (mixed[1] * mixed[2]).astype(BF16)
    pack[pl.ds(0, HALF), :] = prod[pl.ds(rows - HALF, HALF), :]
    for c in range(3):
        pack[pl.ds(HALF + c * TAIL, TAIL), :] = p[c, pl.ds(rows - TAIL, TAIL), :]


def late_kernel(prod, q, mf, skip, fwd, inv, out, spec):
    f = spectrum(fwd[:, pl.ds(0, HALF)], mf[...])
    spec[...] = f
    y = times(spectrum(fwd[...], prod[...]), f)
    skipped = HEAD - HALF
    rows = prod.shape[0] - HEAD
    filtered = dot(inv[pl.ds(skipped, rows), :], y)
    filtered = filtered + skip[...] * prod[pl.ds(HEAD, rows), :].astype(F32)
    out[...] = (q[pl.ds(HEAD, rows), :] * filtered).astype(BF16)


def early_kernel(p, halo, sf, prod, q, late, spec, skip, fwd, inv, one, out, ext, win):
    filt = sf[...].astype(F32)
    mixed = []
    for c in range(3):
        ext[c, pl.ds(0, TAIL), :] = halo[pl.ds(HALF + c * TAIL, TAIL), :].astype(F32)
        ext[c, pl.ds(TAIL, TAIL), :] = p[c, pl.ds(0, TAIL), :].astype(F32)
        mixed.append(taps(ext.at[c], filt[c], TAIL, TAIL))
    win[pl.ds(0, HALF), :] = halo[pl.ds(0, HALF), :]
    win[pl.ds(HALF, TAIL), :] = (mixed[1] * mixed[2]).astype(BF16)
    win[pl.ds(HALF + TAIL, SPAN - TAIL), :] = prod[pl.ds(TAIL, SPAN - TAIL), :]
    f = spec[...]
    first = dot(inv[...], times(spectrum(fwd[...], win[pl.ds(0, SPAN), :]), f))
    second = times(spectrum(fwd[...], win[pl.ds(HALF, SPAN), :]), f)
    second = dot(inv[pl.ds(0, HEAD - HALF), :], second)
    cur = win[pl.ds(HALF, HEAD), :].astype(F32) * skip[...]
    mid = HALF - TAIL
    rest = HEAD - HALF
    pieces = [
        (0, TAIL, mixed[0] * (first[:TAIL] + cur[:TAIL])),
        (TAIL, mid, q[pl.ds(TAIL, mid), :] * (first[TAIL:] + cur[TAIL:HALF])),
        (HALF, rest, q[pl.ds(HALF, rest), :] * (second + cur[HALF:])),
        (HEAD, late.shape[0], late[...]),
    ]
    for at, count, value in pieces:
        value = value.astype(BF16)
        one[pl.ds(at, count), :] = value
        for i in range(out.shape[0]):
            out[i, pl.ds(at, count), :] = value


def arrange_kernel(place, mine, over, *refs):
    arrived, out = refs[:3], refs[3]
    zh, x = place[1], place[3]
    for rel in range(4):
        for other in range(2):
            piece = (mine, over)[other][...] if rel == 0 else arrived[rel - 1][other]
            out[lax.rem(zh + other, 2), lax.rem(x + rel, 4)] = piece


def final_kernel(place, near, far, residual, *refs):
    weights, (out, gv, wv, gsem, wsem) = refs[:16], refs[16:]
    half, y, core = place[0], place[2], place[4]
    gated = [
        pltpu.make_async_copy(near, gv.at[pl.ds(4 * half, 4)], gsem.at[0]),
        pltpu.make_async_copy(far, gv.at[pl.ds(4 * (1 - half), 4)], gsem.at[1]),
    ]
    rows = []
    for i, weight in enumerate(weights):
        target = wv.at[lax.rem(y + i // 2, 8), :, :, lax.rem(core + i % 2, 2)]
        rows.append(pltpu.make_async_copy(weight, target, wsem.at[i]))
    for copy in gated + rows:
        copy.start()
    total = residual[...].astype(F32)
    for copy in gated:
        copy.wait()
    for i in range(8):
        rows[2 * i].wait()
        rows[2 * i + 1].wait()
        k = lax.rem(y + i, 8)
        total = total + dot(gv[k], wv[k].reshape(512, 512))
    out[...] = total.astype(BF16)


def sds(shape, dtype):
    return jax.ShapeDtypeStruct(shape, dtype)


def cost(flops, nbytes):
    return pl.CostEstimate(flops=flops, bytes_accessed=nbytes, transcendentals=0)


def around_y(own):
    up, down, ups, downs = own, own, [], []
    for step in range(4):
        up = lax.ppermute(up, "y", [(i, (i + 1) % 8) for i in range(8)])
        ups.append(up)
        if step < 3:
            down = lax.ppermute(down, "y", [((i + 1) % 8, i) for i in range(8)])
            downs.append(down)
    return [own] + downs + ups[::-1]


def on_device(residual, proj, short_filter, medium_filter, skip, out_weight):
    rows, chans = residual.shape
    fwd, inv = (jnp.asarray(m) for m in dft_matrices())
    p = jnp.transpose(proj, (1, 0, 2))
    sf = jnp.transpose(short_filter, (1, 0, 2))
    skip = skip.reshape(1, chans)
    place = jnp.stack([lax.axis_index(a) for a in ("half", "zh", "y", "x", "core")])
    place = place.astype(jnp.int32)

    over = lax.ppermute(out_weight, "zh", [(0, 1), (1, 0)])

    pack, prod, q = pl.pallas_call(
        local_kernel,
        out_shape=(sds((PACK, chans), BF16), sds((rows, chans), BF16), sds((rows, chans), F32)),
        scratch_shapes=[pltpu.VMEM((3, rows + 8, chans), F32)],
        cost_estimate=cost(6_000_000, 2_000_000),
        name="local",
    )(p, sf)

    halo = lax.ppermute(pack, ("y", "zh", "x", "core"), [(i, i + 1) for i in range(127)])

    late, spec = pl.pallas_call(
        late_kernel,
        out_shape=(sds((rows - HEAD, chans), BF16), sds((SPAN, chans), F32)),
        cost_estimate=cost(300_000_000, 3_000_000),
        name="late",
    )(prod, q, medium_filter, skip, fwd, inv)

    over, late = lax.optimization_barrier((over, late))

    mine = jnp.stack([out_weight, over])
    arrived = []
    for by in (1, 2, 3):
        arrived.append(lax.ppermute(mine, "x", [((i + by) % 4, i) for i in range(4)]))

    gated, copies = pl.pallas_call(
        early_kernel,
        out_shape=(sds((rows, chans), BF16), sds((4, rows, chans), BF16)),
        scratch_shapes=[
            pltpu.VMEM((3, 2 * TAIL, chans), F32),
            pltpu.VMEM((HALF + SPAN, chans), BF16),
        ],
        cost_estimate=cost(600_000_000, 3_000_000),
        name="early",
    )(p, halo, sf, prod, q, late, spec, skip, fwd, inv)

    across = lax.ppermute(gated, "half", [(0, 1), (1, 0)])
    near = lax.all_to_all(copies, "quarter", 0, 0)
    far = lax.all_to_all(jnp.broadcast_to(across, (4, rows, chans)), "quarter", 0, 0)

    smem = pl.BlockSpec(memory_space=pltpu.SMEM)
    vmem = pl.BlockSpec(memory_space=pltpu.VMEM)
    anywhere = pl.BlockSpec(memory_space=pl.ANY)
    block = pl.pallas_call(
        arrange_kernel,
        out_shape=sds((2, 4, WROWS, chans), BF16),
        in_specs=[smem] + [vmem] * 5,
        out_specs=vmem,
        cost_estimate=cost(0, 500_000),
        name="arrange",
    )(place, out_weight, over, *arrived)
    weights = []
    for own in around_y(block):
        weights += [own, lax.ppermute(own, "core", [(0, 1), (1, 0)])]

    return pl.pallas_call(
        final_kernel,
        out_shape=sds((rows, chans), BF16),
        in_specs=[smem, anywhere, anywhere, vmem] + [anywhere] * 16,
        out_specs=vmem,
        scratch_shapes=[
            pltpu.VMEM((8, rows, chans), BF16),
            pltpu.VMEM((8, 2, 4, 2, WROWS, chans), BF16),
            pltpu.SemaphoreType.DMA((2,)),
            pltpu.SemaphoreType.DMA((16,)),
        ],
        cost_estimate=cost(2 * rows * 8 * chans * chans, 8_000_000),
        name="project",
    )(place, near, far, residual, *weights)


def solution(mesh):
    devices = np.asarray(mesh.devices).reshape(8, 2, 4, 2, 2, 4)
    fine = Mesh(devices, ("y", "zh", "x", "core", "half", "quarter"))
    ctx = ("y", "zh", "x", "core")
    tp = ("half", "quarter")
    in_specs = (
        P(ctx, tp),
        P(ctx, None, tp),
        P(None, None, tp),
        P(None, tp),
        P(tp),
        P(ctx, tp),
    )

    return jax.shard_map(
        on_device, mesh=fine, in_specs=in_specs, out_specs=P(ctx, tp), check_vma=False
    )
```

```python
import jax
import jax.numpy as jnp
import numpy as np
from jax import lax
from jax.experimental import pallas as pl
from jax.experimental.pallas import tpu as pltpu
from jax.sharding import Mesh, PartitionSpec as P


SPAN = 256
HALF = 128
HEAD = 144
TAIL = 16
WROWS = 32
PACK = HALF + 3 * TAIL

F32 = jnp.float32
BF16 = jnp.bfloat16


def split(matrix):
    high = matrix.astype(np.float32).astype(BF16)
    low = (matrix - high.astype(np.float64)).astype(np.float32).astype(BF16)
    return high, low


def dft_matrices():
    n = np.arange(SPAN)
    k = np.arange(HALF)[:, None]
    angle = 2.0 * np.pi * ((k * n) % SPAN) / SPAN
    cos, sin = np.cos(angle), np.sin(angle)
    nyquist = np.where(n % 2 == 0, 1.0, -1.0)
    forward = np.concatenate([cos, -sin], 0)
    forward[HALF] = nyquist
    inverse = np.concatenate([2.0 * cos, -2.0 * sin], 0)
    inverse[0] = 1.0
    inverse[HALF] = nyquist
    inverse = inverse.T[HALF:] / SPAN
    fh, fl = split(forward)
    ih, il = split(inverse)
    return np.concatenate([fh, fl], 0), np.concatenate([ih, ih, il], 1)


def dot(a, b):
    return jnp.dot(a, b, preferred_element_type=F32)


def spectrum(forward, values):
    both = dot(forward, values)
    return both[:SPAN] + both[SPAN:]


def times(x, f):
    xr, xi, fr, fi = x[:HALF], x[HALF:], f[:HALF], f[HALF:]
    real = lax.broadcasted_iota(jnp.int32, xr.shape, 0) == 0
    rr, ii = xr * fr, xi * fi
    out_r = jnp.where(real, rr, rr - ii)
    out_i = jnp.where(real, ii, xr * fi + xi * fr)
    y = jnp.concatenate([out_r, out_i], 0)
    high = y.astype(BF16)
    low = (y - high.astype(F32)).astype(BF16)
    return jnp.concatenate([high, low, high], 0)


def taps(ext, filt, start, count):
    total = None
    for j in range(filt.shape[0]):
        term = filt[j : j + 1] * ext[pl.ds(start - j, count), :]
        total = term if total is None else total + term
    return total


def local_kernel(p, sf, pack, prod, q, ext):
    rows = p.shape[1]
    step = 64
    filt = sf[...].astype(F32)
    ext[...] = jnp.zeros_like(ext)
    for c in range(3):
        ext[c, pl.ds(8, rows), :] = p[c].astype(F32)
    for r in reversed(range(0, rows, step)):
        mixed = [taps(ext.at[c], filt[c], 8 + r, step) for c in range(3)]
        q[pl.ds(r, step), :] = mixed[0]
        prod[pl.ds(r, step), :] = (mixed[1] * mixed[2]).astype(BF16)
    pack[pl.ds(0, HALF), :] = prod[pl.ds(rows - HALF, HALF), :]
    for c in range(3):
        pack[pl.ds(HALF + c * TAIL, TAIL), :] = p[c, pl.ds(rows - TAIL, TAIL), :]


def late_kernel(prod, q, mf, skip, fwd, inv, out, spec):
    f = spectrum(fwd[:, pl.ds(0, HALF)], mf[...])
    spec[...] = f
    y = times(spectrum(fwd[...], prod[...]), f)
    skipped = HEAD - HALF
    rows = prod.shape[0] - HEAD
    filtered = dot(inv[pl.ds(skipped, rows), :], y)
    filtered = filtered + skip[...] * prod[pl.ds(HEAD, rows), :].astype(F32)
    out[...] = (q[pl.ds(HEAD, rows), :] * filtered).astype(BF16)


def early_kernel(p, halo, sf, prod, q, late, spec, skip, fwd, inv, out, ext, win):
    filt = sf[...].astype(F32)
    mixed = []
    for c in range(3):
        ext[c, pl.ds(0, TAIL), :] = halo[pl.ds(HALF + c * TAIL, TAIL), :].astype(F32)
        ext[c, pl.ds(TAIL, TAIL), :] = p[c, pl.ds(0, TAIL), :].astype(F32)
        mixed.append(taps(ext.at[c], filt[c], TAIL, TAIL))
    win[pl.ds(0, HALF), :] = halo[pl.ds(0, HALF), :]
    win[pl.ds(HALF, TAIL), :] = (mixed[1] * mixed[2]).astype(BF16)
    win[pl.ds(HALF + TAIL, SPAN - TAIL), :] = prod[pl.ds(TAIL, SPAN - TAIL), :]
    f = spec[...]
    first = dot(inv[...], times(spectrum(fwd[...], win[pl.ds(0, SPAN), :]), f))
    second = times(spectrum(fwd[...], win[pl.ds(HALF, SPAN), :]), f)
    second = dot(inv[pl.ds(0, HEAD - HALF), :], second)
    cur = win[pl.ds(HALF, HEAD), :].astype(F32) * skip[...]
    mid = HALF - TAIL
    rest = HEAD - HALF
    pieces = [
        (0, TAIL, mixed[0] * (first[:TAIL] + cur[:TAIL])),
        (TAIL, mid, q[pl.ds(TAIL, mid), :] * (first[TAIL:] + cur[TAIL:HALF])),
        (HALF, rest, q[pl.ds(HALF, rest), :] * (second + cur[HALF:])),
        (HEAD, late.shape[0], late[...]),
    ]
    for at, count, value in pieces:
        out[pl.ds(at, count), :] = value.astype(BF16)


def arrange_kernel(place, mine, over, *refs):
    arrived, out = refs[:3], refs[3]
    zh, x = place[1], place[3]
    for rel in range(4):
        for other in range(2):
            piece = (mine, over)[other][...] if rel == 0 else arrived[rel - 1][other]
            out[lax.rem(zh + other, 2), lax.rem(x + rel, 4)] = piece


ORDER = ((0, 7, 1), (6, 2), (5, 3, 4))


def final_kernel(place, own, four, two, six, odd, seven, residual, *refs):
    weights, swapped = refs[:8], refs[8:11]
    out, gv, wv, gsem, wsem = refs[11:]
    me, y, core = place[0], place[2], place[4]
    pieces = [(own, 0), (four, 4), (two, 2), (six, 6), (seven, 7)]
    pieces += [(odd.at[i], by) for i, by in enumerate((1, 5, 3))]
    gated = [
        pltpu.make_async_copy(piece, gv.at[lax.bitwise_xor(me, by)], gsem.at[by])
        for piece, by in pieces
    ]
    rows = []
    for batch, order in enumerate(ORDER):
        for i, by in enumerate(order):
            at = lax.rem(y + by, 8)
            rows.append(
                [
                    pltpu.make_async_copy(
                        weights[by], wv.at[at, :, :, core], wsem.at[by, 0]
                    ),
                    pltpu.make_async_copy(
                        swapped[batch].at[i], wv.at[at, :, :, 1 - core], wsem.at[by, 1]
                    ),
                ]
            )
    for copy in gated:
        copy.start()
    for pair in rows:
        for copy in pair:
            copy.start()
    total = residual[...].astype(F32)
    for copy in gated:
        copy.wait()
    for by, pair in zip(sum(ORDER, ()), rows):
        for copy in pair:
            copy.wait()
        k = lax.rem(y + by, 8)
        total = total + dot(gv[k], wv[k].reshape(512, 512))
    out[...] = total.astype(BF16)


def sds(shape, dtype):
    return jax.ShapeDtypeStruct(shape, dtype)


def cost(flops, nbytes):
    return pl.CostEstimate(flops=flops, bytes_accessed=nbytes, transcendentals=0)


def around_y(own):
    up, down, ups, downs = own, own, [], []
    for step in range(4):
        up = lax.ppermute(up, "y", [(i, (i + 1) % 8) for i in range(8)])
        ups.append(up)
        if step < 3:
            down = lax.ppermute(down, "y", [((i + 1) % 8, i) for i in range(8)])
            downs.append(down)
    return [own] + downs + ups[::-1]


def on_device(residual, proj, short_filter, medium_filter, skip, out_weight):
    rows, chans = residual.shape
    fwd, inv = (jnp.asarray(m) for m in dft_matrices())
    p = jnp.transpose(proj, (1, 0, 2))
    sf = jnp.transpose(short_filter, (1, 0, 2))
    skip = skip.reshape(1, chans)
    place = jnp.stack([lax.axis_index(a) for a in ("tp", "zh", "y", "x", "core")])
    place = place.astype(jnp.int32)

    over = lax.ppermute(out_weight, "zh", [(0, 1), (1, 0)])

    pack, prod, q = pl.pallas_call(
        local_kernel,
        out_shape=(sds((PACK, chans), BF16), sds((rows, chans), BF16), sds((rows, chans), F32)),
        scratch_shapes=[pltpu.VMEM((3, rows + 8, chans), F32)],
        cost_estimate=cost(6_000_000, 2_000_000),
        name="local",
    )(p, sf)

    halo = lax.ppermute(pack, ("y", "zh", "x", "core"), [(i, i + 1) for i in range(127)])

    late, spec = pl.pallas_call(
        late_kernel,
        out_shape=(sds((rows - HEAD, chans), BF16), sds((SPAN, chans), F32)),
        cost_estimate=cost(300_000_000, 3_000_000),
        name="late",
    )(prod, q, medium_filter, skip, fwd, inv)

    over, late = lax.optimization_barrier((over, late))

    mine = jnp.stack([out_weight, over])
    arrived = []
    for by in (1, 2, 3):
        arrived.append(lax.ppermute(mine, "x", [((i + by) % 4, i) for i in range(4)]))

    gated = pl.pallas_call(
        early_kernel,
        out_shape=sds((rows, chans), BF16),
        scratch_shapes=[
            pltpu.VMEM((3, 2 * TAIL, chans), F32),
            pltpu.VMEM((HALF + SPAN, chans), BF16),
        ],
        cost_estimate=cost(600_000_000, 3_000_000),
        name="early",
    )(p, halo, sf, prod, q, late, spec, skip, fwd, inv)

    def exchange(piece, by):
        return lax.ppermute(piece, "tp", [(i, i ^ by) for i in range(8)])

    four = exchange(gated, 4)
    two = exchange(gated, 2)
    six = exchange(four, 2)
    odd = exchange(jnp.stack([gated, four, two]), 1)
    seven = exchange(six, 1)

    smem = pl.BlockSpec(memory_space=pltpu.SMEM)
    vmem = pl.BlockSpec(memory_space=pltpu.VMEM)
    anywhere = pl.BlockSpec(memory_space=pl.ANY)
    block = pl.pallas_call(
        arrange_kernel,
        out_shape=sds((2, 4, WROWS, chans), BF16),
        in_specs=[smem] + [vmem] * 5,
        out_specs=vmem,
        cost_estimate=cost(0, 500_000),
        name="arrange",
    )(place, out_weight, over, *arrived)
    weights = around_y(block)
    swapped = []
    for order in ORDER:
        group = jnp.stack([weights[by] for by in order])
        swapped.append(lax.ppermute(group, "core", [(0, 1), (1, 0)]))

    return pl.pallas_call(
        final_kernel,
        out_shape=sds((rows, chans), BF16),
        in_specs=[smem] + [anywhere] * 6 + [vmem] + [anywhere] * 11,
        out_specs=vmem,
        scratch_shapes=[
            pltpu.VMEM((8, rows, chans), BF16),
            pltpu.VMEM((8, 2, 4, 2, WROWS, chans), BF16),
            pltpu.SemaphoreType.DMA((8,)),
            pltpu.SemaphoreType.DMA((8, 2)),
        ],
        cost_estimate=cost(2 * rows * 8 * chans * chans, 8_000_000),
        name="project",
    )(place, gated, four, two, six, odd, seven, residual, *weights, *swapped)


def solution(mesh):
    devices = np.asarray(mesh.devices).reshape(8, 2, 4, 2, 8)
    fine = Mesh(devices, ("y", "zh", "x", "core", "tp"))
    ctx = ("y", "zh", "x", "core")
    tp = "tp"
    in_specs = (
        P(ctx, tp),
        P(ctx, None, tp),
        P(None, None, tp),
        P(None, tp),
        P(tp),
        P(ctx, tp),
    )

    return jax.shard_map(
        on_device, mesh=fine, in_specs=in_specs, out_specs=P(ctx, tp), check_vma=False
    )
```

```python
import functools

import jax
import jax.numpy as jnp
import numpy as np
from jax import lax
from jax.experimental import pallas as pl
from jax.experimental.pallas import tpu as pltpu
from jax.sharding import Mesh, PartitionSpec as P


SPAN = 256
HALF = 128
HEAD = 144
TAIL = 16
WROWS = 32
PACK = HALF + 3 * TAIL

F32 = jnp.float32
BF16 = jnp.bfloat16


def split(matrix):
    high = matrix.astype(np.float32).astype(BF16)
    low = (matrix - high.astype(np.float64)).astype(np.float32).astype(BF16)
    return high, low


def dft_matrices():
    n = np.arange(SPAN)
    k = np.arange(HALF)[:, None]
    angle = 2.0 * np.pi * ((k * n) % SPAN) / SPAN
    cos, sin = np.cos(angle), np.sin(angle)
    nyquist = np.where(n % 2 == 0, 1.0, -1.0)
    forward = np.concatenate([cos, -sin], 0)
    forward[HALF] = nyquist
    inverse = np.concatenate([2.0 * cos, -2.0 * sin], 0)
    inverse[0] = 1.0
    inverse[HALF] = nyquist
    inverse = inverse.T[HALF:] / SPAN
    fh, fl = split(forward)
    ih, il = split(inverse)
    return np.concatenate([fh, fl], 0), np.concatenate([ih, ih, il], 1)


def dot(a, b):
    return jnp.dot(a, b, preferred_element_type=F32)


def spectrum(forward, values):
    both = dot(forward, values)
    return both[:SPAN] + both[SPAN:]


def times(x, f):
    xr, xi, fr, fi = x[:HALF], x[HALF:], f[:HALF], f[HALF:]
    real = lax.broadcasted_iota(jnp.int32, xr.shape, 0) == 0
    rr, ii = xr * fr, xi * fi
    out_r = jnp.where(real, rr, rr - ii)
    out_i = jnp.where(real, ii, xr * fi + xi * fr)
    y = jnp.concatenate([out_r, out_i], 0)
    high = y.astype(BF16)
    low = (y - high.astype(F32)).astype(BF16)
    return jnp.concatenate([high, low, high], 0)


def taps(ext, filt, start, count):
    total = None
    for j in range(filt.shape[0]):
        term = filt[j : j + 1] * ext[pl.ds(start - j, count), :]
        total = term if total is None else total + term
    return total


def local_kernel(p, sf, pack, prod, q, ext):
    rows = p.shape[1]
    step = 64
    filt = sf[...].astype(F32)
    ext[...] = jnp.zeros_like(ext)
    for c in range(3):
        ext[c, pl.ds(8, rows), :] = p[c].astype(F32)
    for r in reversed(range(0, rows, step)):
        mixed = [taps(ext.at[c], filt[c], 8 + r, step) for c in range(3)]
        q[pl.ds(r, step), :] = mixed[0]
        prod[pl.ds(r, step), :] = (mixed[1] * mixed[2]).astype(BF16)
    pack[pl.ds(0, HALF), :] = prod[pl.ds(rows - HALF, HALF), :]
    for c in range(3):
        pack[pl.ds(HALF + c * TAIL, TAIL), :] = p[c, pl.ds(rows - TAIL, TAIL), :]


def late_kernel(prod, q, mf, skip, fwd, inv, out, spec):
    f = spectrum(fwd[:, pl.ds(0, HALF)], mf[...])
    spec[...] = f
    y = times(spectrum(fwd[...], prod[...]), f)
    skipped = HEAD - HALF
    rows = prod.shape[0] - HEAD
    filtered = dot(inv[pl.ds(skipped, rows), :], y)
    filtered = filtered + skip[...] * prod[pl.ds(HEAD, rows), :].astype(F32)
    out[...] = (q[pl.ds(HEAD, rows), :] * filtered).astype(BF16)


def early_kernel(p, halo, sf, prod, q, late, spec, skip, fwd, inv, out, ext, win):
    filt = sf[...].astype(F32)
    mixed = []
    for c in range(3):
        ext[c, pl.ds(0, TAIL), :] = halo[pl.ds(HALF + c * TAIL, TAIL), :].astype(F32)
        ext[c, pl.ds(TAIL, TAIL), :] = p[c, pl.ds(0, TAIL), :].astype(F32)
        mixed.append(taps(ext.at[c], filt[c], TAIL, TAIL))
    win[pl.ds(0, HALF), :] = halo[pl.ds(0, HALF), :]
    win[pl.ds(HALF, TAIL), :] = (mixed[1] * mixed[2]).astype(BF16)
    win[pl.ds(HALF + TAIL, SPAN - TAIL), :] = prod[pl.ds(TAIL, SPAN - TAIL), :]
    f = spec[...]
    first = dot(inv[...], times(spectrum(fwd[...], win[pl.ds(0, SPAN), :]), f))
    second = times(spectrum(fwd[...], win[pl.ds(HALF, SPAN), :]), f)
    second = dot(inv[pl.ds(0, HEAD - HALF), :], second)
    cur = win[pl.ds(HALF, HEAD), :].astype(F32) * skip[...]
    mid = HALF - TAIL
    rest = HEAD - HALF
    pieces = [
        (0, TAIL, mixed[0] * (first[:TAIL] + cur[:TAIL])),
        (TAIL, mid, q[pl.ds(TAIL, mid), :] * (first[TAIL:] + cur[TAIL:HALF])),
        (HALF, rest, q[pl.ds(HALF, rest), :] * (second + cur[HALF:])),
        (HEAD, late.shape[0], late[...]),
    ]
    for at, count, value in pieces:
        out[pl.ds(at, count), :] = value.astype(BF16)


ORDER = ((0, 7, 1), (6, 2, 4), (5, 3))


def project_kernel(batches, place, *refs):
    pieces = refs[:6]
    count = sum(len(ORDER[batch]) for batch in batches)
    weights = refs[6 : 6 + count]
    swapped = refs[6 + count : 6 + count + len(batches)]
    start, out, gv, wv, gsem, wsem = refs[6 + count + len(batches) :]
    me, y, x, core = place[0], place[2], place[3], place[4]
    own, four, two, six, odd, seven = pieces
    gated = [(own, 0), (four, 4), (two, 2), (six, 6), (seven, 7)]
    gated += [(odd.at[i], by) for i, by in enumerate((1, 5, 3))]
    gated = [
        pltpu.make_async_copy(piece, gv.at[lax.bitwise_xor(me, by)], gsem.at[by])
        for piece, by in gated
    ]
    places = [(batch, i) for batch in batches for i in range(len(ORDER[batch]))]
    blocks = []
    for n, (batch, i) in enumerate(places):
        parts = []
        for rel in range(4):
            at = lax.rem(x + rel, 4)
            for other, source in enumerate((weights[n], swapped[batches.index(batch)].at[i])):
                to = core if other == 0 else 1 - core
                parts.append(
                    pltpu.make_async_copy(
                        source.at[rel], wv.at[n, :, at, to], wsem.at[n, rel * 2 + other]
                    )
                )
        blocks.append(parts)
    for copy in gated + sum(blocks, []):
        copy.start()
    total = start[...].astype(F32)
    for copy in gated:
        copy.wait()
    for n, (batch, i) in enumerate(places):
        for copy in blocks[n]:
            copy.wait()
        k = lax.rem(y + ORDER[batch][i], 8)
        total = total + dot(gv[k], wv[n].reshape(512, 512))
    out[...] = total.astype(out.dtype)


def sds(shape, dtype):
    return jax.ShapeDtypeStruct(shape, dtype)


def cost(flops, nbytes):
    return pl.CostEstimate(flops=flops, bytes_accessed=nbytes, transcendentals=0)


def around_y(own):
    def shift(piece, by):
        return lax.ppermute(piece, "y", [((i + by) % 8, i) for i in range(8)])

    up, down, ups, downs = own, own, [], []
    for _ in range(3):
        up, down = shift(up, 7), shift(down, 1)
        ups.append(up)
        downs.append(down)
    return [own] + downs + [shift(own, 4)] + ups[::-1]


def on_device(residual, proj, short_filter, medium_filter, skip, out_weight):
    rows, chans = residual.shape
    fwd, inv = (jnp.asarray(m) for m in dft_matrices())
    p = jnp.transpose(proj, (1, 0, 2))
    sf = jnp.transpose(short_filter, (1, 0, 2))
    skip = skip.reshape(1, chans)
    place = jnp.stack([lax.axis_index(a) for a in ("tp", "zh", "y", "x", "core")])
    place = place.astype(jnp.int32)

    over = lax.ppermute(out_weight, "zh", [(0, 1), (1, 0)])

    pack, prod, q = pl.pallas_call(
        local_kernel,
        out_shape=(sds((PACK, chans), BF16), sds((rows, chans), BF16), sds((rows, chans), F32)),
        scratch_shapes=[pltpu.VMEM((3, rows + 8, chans), F32)],
        cost_estimate=cost(6_000_000, 2_000_000),
        name="local",
    )(p, sf)

    halo = lax.ppermute(pack, ("y", "zh", "x", "core"), [(i, i + 1) for i in range(127)])

    late, spec = pl.pallas_call(
        late_kernel,
        out_shape=(sds((rows - HEAD, chans), BF16), sds((SPAN, chans), F32)),
        cost_estimate=cost(300_000_000, 3_000_000),
        name="late",
    )(prod, q, medium_filter, skip, fwd, inv)

    over, late = lax.optimization_barrier((over, late))

    mine = jnp.where(
        lax.axis_index("zh") == 0,
        jnp.stack([out_weight, over]),
        jnp.stack([over, out_weight]),
    )
    arrived = []
    for by in (1, 2, 3):
        arrived.append(lax.ppermute(mine, "x", [((i + by) % 4, i) for i in range(4)]))

    gated = pl.pallas_call(
        early_kernel,
        out_shape=sds((rows, chans), BF16),
        scratch_shapes=[
            pltpu.VMEM((3, 2 * TAIL, chans), F32),
            pltpu.VMEM((HALF + SPAN, chans), BF16),
        ],
        cost_estimate=cost(600_000_000, 3_000_000),
        name="early",
    )(p, halo, sf, prod, q, late, spec, skip, fwd, inv)

    def exchange(piece, by):
        return lax.ppermute(piece, "tp", [(i, i ^ by) for i in range(8)])

    four = exchange(gated, 4)
    two = exchange(gated, 2)
    six = exchange(four, 2)
    odd = exchange(jnp.stack([gated, four, two]), 1)
    seven = exchange(six, 1)

    smem = pl.BlockSpec(memory_space=pltpu.SMEM)
    vmem = pl.BlockSpec(memory_space=pltpu.VMEM)
    anywhere = pl.BlockSpec(memory_space=pl.ANY)
    block = jnp.stack([mine] + arrived)
    weights = around_y(block)
    swapped = []
    for order in ORDER:
        group = jnp.stack([weights[by] for by in order])
        swapped.append(lax.ppermute(group, "core", [(0, 1), (1, 0)]))

    def project(batches, start, dtype):
        count = sum(len(ORDER[batch]) for batch in batches)
        used = [weights[by] for batch in batches for by in ORDER[batch]]
        used += [swapped[batch] for batch in batches]
        return pl.pallas_call(
            functools.partial(project_kernel, batches),
            out_shape=sds((rows, chans), dtype),
            in_specs=[smem] + [anywhere] * (6 + len(used)) + [vmem],
            out_specs=vmem,
            scratch_shapes=[
                pltpu.VMEM((8, rows, chans), BF16),
                pltpu.VMEM((count, 2, 4, 2, WROWS, chans), BF16),
                pltpu.SemaphoreType.DMA((8,)),
                pltpu.SemaphoreType.DMA((count, 8)),
            ],
            cost_estimate=cost(2 * rows * count * chans * chans, 8_000_000),
            name="project",
        )(place, gated, four, two, six, odd, seven, *used, start)

    most = project((0, 1), residual, F32)
    return project((2,), most, BF16)


def solution(mesh):
    devices = np.asarray(mesh.devices).reshape(8, 2, 4, 2, 8)
    fine = Mesh(devices, ("y", "zh", "x", "core", "tp"))
    ctx = ("y", "zh", "x", "core")
    tp = "tp"
    in_specs = (
        P(ctx, tp),
        P(ctx, None, tp),
        P(None, None, tp),
        P(None, tp),
        P(tp),
        P(ctx, tp),
    )

    return jax.shard_map(
        on_device, mesh=fine, in_specs=in_specs, out_specs=P(ctx, tp), check_vma=False
    )
```

```python
import jax
import jax.numpy as jnp
import numpy as np
from jax import lax
from jax.experimental import pallas as pl
from jax.experimental.pallas import tpu as pltpu
from jax.sharding import Mesh, PartitionSpec as P


SPAN = 256
HALF = 128
HEAD = 144
TAIL = 16
PACK = HALF + 3 * TAIL

F32 = jnp.float32
BF16 = jnp.bfloat16


def split(matrix):
    high = matrix.astype(np.float32).astype(BF16)
    low = (matrix - high.astype(np.float64)).astype(np.float32).astype(BF16)
    return high, low


def dft_matrices():
    n = np.arange(SPAN)
    k = np.arange(HALF)[:, None]
    angle = 2.0 * np.pi * ((k * n) % SPAN) / SPAN
    cos, sin = np.cos(angle), np.sin(angle)
    nyquist = np.where(n % 2 == 0, 1.0, -1.0)
    forward = np.concatenate([cos, -sin], 0)
    forward[HALF] = nyquist
    inverse = np.concatenate([2.0 * cos, -2.0 * sin], 0)
    inverse[0] = 1.0
    inverse[HALF] = nyquist
    inverse = inverse.T[HALF:] / SPAN
    fh, fl = split(forward)
    ih, il = split(inverse)
    return np.concatenate([fh, fl], 0), np.concatenate([ih, ih, il], 1)


def dot(a, b):
    return jnp.dot(a, b, preferred_element_type=F32)


def spectrum(forward, values):
    both = dot(forward, values)
    return both[:SPAN] + both[SPAN:]


def times(x, f):
    xr, xi, fr, fi = x[:HALF], x[HALF:], f[:HALF], f[HALF:]
    real = lax.broadcasted_iota(jnp.int32, xr.shape, 0) == 0
    rr, ii = xr * fr, xi * fi
    out_r = jnp.where(real, rr, rr - ii)
    out_i = jnp.where(real, ii, xr * fi + xi * fr)
    y = jnp.concatenate([out_r, out_i], 0)
    high = y.astype(BF16)
    low = (y - high.astype(F32)).astype(BF16)
    return jnp.concatenate([high, low, high], 0)


def taps(ext, filt, start, count):
    total = None
    for j in range(filt.shape[0]):
        term = filt[j : j + 1] * ext[pl.ds(start - j, count), :]
        total = term if total is None else total + term
    return total


def local_kernel(p, sf, pack, prod, q, ext):
    rows = p.shape[1]
    step = 64
    filt = sf[...].astype(F32)
    ext[...] = jnp.zeros_like(ext)
    for c in range(3):
        ext[c, pl.ds(8, rows), :] = p[c].astype(F32)
    for r in reversed(range(0, rows, step)):
        mixed = [taps(ext.at[c], filt[c], 8 + r, step) for c in range(3)]
        q[pl.ds(r, step), :] = mixed[0]
        prod[pl.ds(r, step), :] = (mixed[1] * mixed[2]).astype(BF16)
    pack[pl.ds(0, HALF), :] = prod[pl.ds(rows - HALF, HALF), :]
    for c in range(3):
        pack[pl.ds(HALF + c * TAIL, TAIL), :] = p[c, pl.ds(rows - TAIL, TAIL), :]


def late_kernel(prod, q, mf, skip, fwd, inv, out, spec):
    f = spectrum(fwd[:, pl.ds(0, HALF)], mf[...])
    spec[...] = f
    y = times(spectrum(fwd[...], prod[...]), f)
    skipped = HEAD - HALF
    rows = prod.shape[0] - HEAD
    filtered = dot(inv[pl.ds(skipped, rows), :], y)
    filtered = filtered + skip[...] * prod[pl.ds(HEAD, rows), :].astype(F32)
    out[...] = (q[pl.ds(HEAD, rows), :] * filtered).astype(BF16)


def early_kernel(p, halo, sf, prod, q, late, spec, skip, fwd, inv, out, ext, win):
    filt = sf[...].astype(F32)
    mixed = []
    for c in range(3):
        ext[c, pl.ds(0, TAIL), :] = halo[pl.ds(HALF + c * TAIL, TAIL), :].astype(F32)
        ext[c, pl.ds(TAIL, TAIL), :] = p[c, pl.ds(0, TAIL), :].astype(F32)
        mixed.append(taps(ext.at[c], filt[c], TAIL, TAIL))
    win[pl.ds(0, HALF), :] = halo[pl.ds(0, HALF), :]
    win[pl.ds(HALF, TAIL), :] = (mixed[1] * mixed[2]).astype(BF16)
    win[pl.ds(HALF + TAIL, SPAN - TAIL), :] = prod[pl.ds(TAIL, SPAN - TAIL), :]
    f = spec[...]
    first = dot(inv[...], times(spectrum(fwd[...], win[pl.ds(0, SPAN), :]), f))
    second = times(spectrum(fwd[...], win[pl.ds(HALF, SPAN), :]), f)
    second = dot(inv[pl.ds(0, HEAD - HALF), :], second)
    cur = win[pl.ds(HALF, HEAD), :].astype(F32) * skip[...]
    mid = HALF - TAIL
    rest = HEAD - HALF
    pieces = [
        (0, TAIL, mixed[0] * (first[:TAIL] + cur[:TAIL])),
        (TAIL, mid, q[pl.ds(TAIL, mid), :] * (first[TAIL:] + cur[TAIL:HALF])),
        (HALF, rest, q[pl.ds(HALF, rest), :] * (second + cur[HALF:])),
        (HEAD, late.shape[0], late[...]),
    ]
    for at, count, value in pieces:
        out[pl.ds(at, count), :] = value.astype(BF16)


FIRST = (0, 7, 1, 6, 2)
LAST = (5, 3, 4)


def most_kernel(place, own, four, two, six, odd, seven, residual, *refs):
    weights, (out, kept, gv, wv, gsem, wsem) = refs[:5], refs[5:]
    me, y = place[0], place[1]
    pieces = [(own, 0), (four, 4), (two, 2), (six, 6), (seven, 7)]
    pieces += [(odd.at[i], by) for i, by in enumerate((1, 5, 3))]
    gated = [
        pltpu.make_async_copy(piece, gv.at[lax.bitwise_xor(me, by)], gsem.at[by])
        for piece, by in pieces
    ]
    rows = [pltpu.make_async_copy(w, wv.at[n], wsem.at[n]) for n, w in enumerate(weights)]
    for copy in gated + rows:
        copy.start()
    total = residual[...].astype(F32)
    for copy in gated:
        copy.wait()
    for n, by in enumerate(LAST):
        kept[n] = gv[lax.rem(y + by, 8)]
    for n, by in enumerate(FIRST):
        rows[n].wait()
        total = total + dot(gv[lax.rem(y + by, 8)], wv[n])
    out[...] = total


def rest_kernel(start, kept, *refs):
    weights, (out, wv, wsem) = refs[:3], refs[3:]
    rows = [pltpu.make_async_copy(w, wv.at[n], wsem.at[n]) for n, w in enumerate(weights)]
    for copy in rows:
        copy.start()
    total = start[...]
    for n, copy in enumerate(rows):
        copy.wait()
        total = total + dot(kept[n], wv[n])
    out[...] = total.astype(BF16)


def sds(shape, dtype):
    return jax.ShapeDtypeStruct(shape, dtype)


def cost(flops, nbytes):
    return pl.CostEstimate(flops=flops, bytes_accessed=nbytes, transcendentals=0)


def around_y(own):
    def shift(piece, by):
        return lax.ppermute(piece, "y", [((i + by) % 8, i) for i in range(8)])

    blocks = {0: own}
    for step in range(4):
        blocks[7 - step] = shift(blocks[(8 - step) % 8], 7)
        if step < 3:
            blocks[step + 1] = shift(blocks[step], 1)
    return blocks


def on_device(residual, proj, short_filter, medium_filter, skip, out_weight):
    rows, chans = residual.shape
    fwd, inv = (jnp.asarray(m) for m in dft_matrices())
    p = jnp.transpose(proj, (1, 0, 2))
    sf = jnp.transpose(short_filter, (1, 0, 2))
    skip = skip.reshape(1, chans)
    place = jnp.stack([lax.axis_index("tp"), lax.axis_index("y")]).astype(jnp.int32)

    mine = jnp.broadcast_to(out_weight, (16,) + out_weight.shape)
    block = lax.all_to_all(mine, ("zh", "x", "core"), 0, 0).reshape(chans, chans)

    pack, prod, q = pl.pallas_call(
        local_kernel,
        out_shape=(sds((PACK, chans), BF16), sds((rows, chans), BF16), sds((rows, chans), F32)),
        scratch_shapes=[pltpu.VMEM((3, rows + 8, chans), F32)],
        cost_estimate=cost(6_000_000, 2_000_000),
        name="local",
    )(p, sf)

    halo = lax.ppermute(pack, ("y", "zh", "x", "core"), [(i, i + 1) for i in range(127)])

    late, spec = pl.pallas_call(
        late_kernel,
        out_shape=(sds((rows - HEAD, chans), BF16), sds((SPAN, chans), F32)),
        cost_estimate=cost(300_000_000, 3_000_000),
        name="late",
    )(prod, q, medium_filter, skip, fwd, inv)

    gated = pl.pallas_call(
        early_kernel,
        out_shape=sds((rows, chans), BF16),
        scratch_shapes=[
            pltpu.VMEM((3, 2 * TAIL, chans), F32),
            pltpu.VMEM((HALF + SPAN, chans), BF16),
        ],
        cost_estimate=cost(600_000_000, 3_000_000),
        name="early",
    )(p, halo, sf, prod, q, late, spec, skip, fwd, inv)

    def exchange(piece, by):
        return lax.ppermute(piece, "tp", [(i, i ^ by) for i in range(8)])

    four = exchange(gated, 4)
    two = exchange(gated, 2)
    six = exchange(four, 2)
    odd = exchange(jnp.stack([gated, four, two]), 1)
    seven = exchange(six, 1)

    smem = pl.BlockSpec(memory_space=pltpu.SMEM)
    vmem = pl.BlockSpec(memory_space=pltpu.VMEM)
    anywhere = pl.BlockSpec(memory_space=pl.ANY)
    weights = around_y(block)
    most, kept = pl.pallas_call(
        most_kernel,
        out_shape=(sds((rows, chans), F32), sds((3, rows, chans), BF16)),
        in_specs=[smem] + [anywhere] * 6 + [vmem] + [anywhere] * 5,
        out_specs=(vmem, vmem),
        scratch_shapes=[
            pltpu.VMEM((8, rows, chans), BF16),
            pltpu.VMEM((5, chans, chans), BF16),
            pltpu.SemaphoreType.DMA((8,)),
            pltpu.SemaphoreType.DMA((5,)),
        ],
        cost_estimate=cost(10 * rows * chans * chans, 6_000_000),
        name="most",
    )(place, gated, four, two, six, odd, seven, residual, *[weights[i] for i in FIRST])
    return pl.pallas_call(
        rest_kernel,
        out_shape=sds((rows, chans), BF16),
        in_specs=[vmem, vmem] + [anywhere] * 3,
        out_specs=vmem,
        scratch_shapes=[
            pltpu.VMEM((3, chans, chans), BF16),
            pltpu.SemaphoreType.DMA((3,)),
        ],
        cost_estimate=cost(6 * rows * chans * chans, 3_000_000),
        name="rest",
    )(most, kept, *[weights[i] for i in LAST])


def solution(mesh):
    devices = np.asarray(mesh.devices).reshape(8, 2, 4, 2, 8)
    fine = Mesh(devices, ("y", "zh", "x", "core", "tp"))
    ctx = ("y", "zh", "x", "core")
    tp = "tp"
    in_specs = (
        P(ctx, tp),
        P(ctx, None, tp),
        P(None, None, tp),
        P(None, tp),
        P(tp),
        P(ctx, tp),
    )

    return jax.shard_map(
        on_device, mesh=fine, in_specs=in_specs, out_specs=P(ctx, tp), check_vma=False
    )
```

```python
import functools

import jax
import jax.numpy as jnp
import numpy as np
from jax import lax
from jax.experimental import pallas as pl
from jax.experimental.pallas import tpu as pltpu
from jax.sharding import Mesh, PartitionSpec as P


SPAN = 256
HALF = 128
HEAD = 144
TAIL = 16
WROWS = 32
PACK = HALF + 3 * TAIL

F32 = jnp.float32
BF16 = jnp.bfloat16


def split(matrix):
    high = matrix.astype(np.float32).astype(BF16)
    low = (matrix - high.astype(np.float64)).astype(np.float32).astype(BF16)
    return high, low


def dft_matrices():
    n = np.arange(SPAN)
    k = np.arange(HALF)[:, None]
    angle = 2.0 * np.pi * ((k * n) % SPAN) / SPAN
    cos, sin = np.cos(angle), np.sin(angle)
    nyquist = np.where(n % 2 == 0, 1.0, -1.0)
    forward = np.concatenate([cos, -sin], 0)
    forward[HALF] = nyquist
    inverse = np.concatenate([2.0 * cos, -2.0 * sin], 0)
    inverse[0] = 1.0
    inverse[HALF] = nyquist
    inverse = inverse.T[HALF:] / SPAN
    fh, fl = split(forward)
    ih, il = split(inverse)
    return np.concatenate([fh, fl], 0), np.concatenate([ih, ih, il], 1)


def dot(a, b):
    return jnp.dot(a, b, preferred_element_type=F32)


def spectrum(forward, values):
    both = dot(forward, values)
    return both[:SPAN] + both[SPAN:]


def times(x, f):
    xr, xi, fr, fi = x[:HALF], x[HALF:], f[:HALF], f[HALF:]
    real = lax.broadcasted_iota(jnp.int32, xr.shape, 0) == 0
    rr, ii = xr * fr, xi * fi
    out_r = jnp.where(real, rr, rr - ii)
    out_i = jnp.where(real, ii, xr * fi + xi * fr)
    y = jnp.concatenate([out_r, out_i], 0)
    high = y.astype(BF16)
    low = (y - high.astype(F32)).astype(BF16)
    return jnp.concatenate([high, low, high], 0)


def taps(ext, filt, start, count):
    total = None
    for j in range(filt.shape[0]):
        term = filt[j : j + 1] * ext[pl.ds(start - j, count), :]
        total = term if total is None else total + term
    return total


def local_kernel(p, sf, pack, prod, q, ext):
    rows = p.shape[1]
    step = 64
    filt = sf[...].astype(F32)
    ext[...] = jnp.zeros_like(ext)
    for c in range(3):
        ext[c, pl.ds(8, rows), :] = p[c].astype(F32)
    for r in reversed(range(0, rows, step)):
        mixed = [taps(ext.at[c], filt[c], 8 + r, step) for c in range(3)]
        q[pl.ds(r, step), :] = mixed[0]
        prod[pl.ds(r, step), :] = (mixed[1] * mixed[2]).astype(BF16)
    pack[pl.ds(0, HALF), :] = prod[pl.ds(rows - HALF, HALF), :]
    for c in range(3):
        pack[pl.ds(HALF + c * TAIL, TAIL), :] = p[c, pl.ds(rows - TAIL, TAIL), :]


def late_kernel(prod, q, mf, skip, fwd, inv, out, spec):
    f = spectrum(fwd[:, pl.ds(0, HALF)], mf[...])
    spec[...] = f
    y = times(spectrum(fwd[...], prod[...]), f)
    skipped = HEAD - HALF
    rows = prod.shape[0] - HEAD
    filtered = dot(inv[pl.ds(skipped, rows), :], y)
    filtered = filtered + skip[...] * prod[pl.ds(HEAD, rows), :].astype(F32)
    out[...] = (q[pl.ds(HEAD, rows), :] * filtered).astype(BF16)


def early_kernel(p, halo, sf, prod, q, late, spec, skip, fwd, inv, out, ext, win):
    filt = sf[...].astype(F32)
    mixed = []
    for c in range(3):
        ext[c, pl.ds(0, TAIL), :] = halo[pl.ds(HALF + c * TAIL, TAIL), :].astype(F32)
        ext[c, pl.ds(TAIL, TAIL), :] = p[c, pl.ds(0, TAIL), :].astype(F32)
        mixed.append(taps(ext.at[c], filt[c], TAIL, TAIL))
    win[pl.ds(0, HALF), :] = halo[pl.ds(0, HALF), :]
    win[pl.ds(HALF, TAIL), :] = (mixed[1] * mixed[2]).astype(BF16)
    win[pl.ds(HALF + TAIL, SPAN - TAIL), :] = prod[pl.ds(TAIL, SPAN - TAIL), :]
    f = spec[...]
    first = dot(inv[...], times(spectrum(fwd[...], win[pl.ds(0, SPAN), :]), f))
    second = times(spectrum(fwd[...], win[pl.ds(HALF, SPAN), :]), f)
    second = dot(inv[pl.ds(0, HEAD - HALF), :], second)
    cur = win[pl.ds(HALF, HEAD), :].astype(F32) * skip[...]
    mid = HALF - TAIL
    rest = HEAD - HALF
    pieces = [
        (0, TAIL, mixed[0] * (first[:TAIL] + cur[:TAIL])),
        (TAIL, mid, q[pl.ds(TAIL, mid), :] * (first[TAIL:] + cur[TAIL:HALF])),
        (HALF, rest, q[pl.ds(HALF, rest), :] * (second + cur[HALF:])),
        (HEAD, late.shape[0], late[...]),
    ]
    for at, count, value in pieces:
        out[pl.ds(at, count), :] = value.astype(BF16)


ORDER = ((0, 7, 1), (6, 2, 4), (5, 3))


def project_kernel(batches, place, *refs):
    pieces = refs[:6]
    count = sum(len(ORDER[batch]) for batch in batches)
    weights = refs[6 : 6 + count]
    swapped = refs[6 + count : 6 + count + len(batches)]
    start, out, gv, wv, gsem, wsem = refs[6 + count + len(batches) :]
    me, y, x, core = place[0], place[2], place[3], place[4]
    own, four, two, six, odd, seven = pieces
    gated = [(own, 0), (four, 4), (two, 2), (six, 6), (seven, 7)]
    gated += [(odd.at[i], by) for i, by in enumerate((1, 5, 3))]
    gated = [
        pltpu.make_async_copy(piece, gv.at[lax.bitwise_xor(me, by)], gsem.at[by])
        for piece, by in gated
    ]
    places = [(batch, i) for batch in batches for i in range(len(ORDER[batch]))]
    blocks = []
    for n, (batch, i) in enumerate(places):
        parts = []
        for rel in range(4):
            at = lax.rem(x + rel, 4)
            for other, source in enumerate((weights[n], swapped[batches.index(batch)].at[i])):
                to = core if other == 0 else 1 - core
                parts.append(
                    pltpu.make_async_copy(
                        source.at[rel], wv.at[n, :, at, to], wsem.at[n, rel * 2 + other]
                    )
                )
        blocks.append(parts)
    for copy in gated + sum(blocks, []):
        copy.start()
    total = start[...].astype(F32)
    for copy in gated:
        copy.wait()
    for n, (batch, i) in enumerate(places):
        for copy in blocks[n]:
            copy.wait()
        k = lax.rem(y + ORDER[batch][i], 8)
        total = total + dot(gv[k], wv[n].reshape(512, 512))
    out[...] = total.astype(out.dtype)


def sds(shape, dtype):
    return jax.ShapeDtypeStruct(shape, dtype)


def cost(flops, nbytes):
    return pl.CostEstimate(flops=flops, bytes_accessed=nbytes, transcendentals=0)


def around_y(own):
    def shift(piece, by):
        return lax.ppermute(piece, "y", [((i + by) % 8, i) for i in range(8)])

    up, down, ups, downs = own, own, [], []
    for _ in range(3):
        up, down = shift(up, 7), shift(down, 1)
        ups.append(up)
        downs.append(down)
    return [own] + downs + [shift(own, 4)] + ups[::-1]


def on_device(residual, proj, short_filter, medium_filter, skip, out_weight):
    rows, chans = residual.shape
    fwd, inv = (jnp.asarray(m) for m in dft_matrices())
    p = jnp.transpose(proj, (1, 0, 2))
    sf = jnp.transpose(short_filter, (1, 0, 2))
    skip = skip.reshape(1, chans)
    place = jnp.stack([lax.axis_index(a) for a in ("tp", "zh", "y", "x", "core")])
    place = place.astype(jnp.int32)

    over = lax.ppermute(out_weight, "zh", [(0, 1), (1, 0)])

    pack, prod, q = pl.pallas_call(
        local_kernel,
        out_shape=(sds((PACK, chans), BF16), sds((rows, chans), BF16), sds((rows, chans), F32)),
        scratch_shapes=[pltpu.VMEM((3, rows + 8, chans), F32)],
        cost_estimate=cost(6_000_000, 2_000_000),
        name="local",
    )(p, sf)

    halo = lax.ppermute(pack, ("y", "zh", "x", "core"), [(i, i + 1) for i in range(127)])

    late, spec = pl.pallas_call(
        late_kernel,
        out_shape=(sds((rows - HEAD, chans), BF16), sds((SPAN, chans), F32)),
        cost_estimate=cost(300_000_000, 3_000_000),
        name="late",
    )(prod, q, medium_filter, skip, fwd, inv)

    over, late, place = lax.optimization_barrier((over, late, place))

    mine = jnp.where(
        lax.axis_index("zh") == 0,
        jnp.stack([out_weight, over]),
        jnp.stack([over, out_weight]),
    )
    arrived = []
    for by in (1, 2, 3):
        arrived.append(lax.ppermute(mine, "x", [((i + by) % 4, i) for i in range(4)]))

    gated = pl.pallas_call(
        early_kernel,
        out_shape=sds((rows, chans), BF16),
        scratch_shapes=[
            pltpu.VMEM((3, 2 * TAIL, chans), F32),
            pltpu.VMEM((HALF + SPAN, chans), BF16),
        ],
        cost_estimate=cost(600_000_000, 3_000_000),
        name="early",
    )(p, halo, sf, prod, q, late, spec, skip, fwd, inv)

    def exchange(piece, by):
        return lax.ppermute(piece, "tp", [(i, i ^ by) for i in range(8)])

    four = exchange(gated, 4)
    two = exchange(gated, 2)
    six = exchange(four, 2)
    odd = exchange(jnp.stack([gated, four, two]), 1)
    seven = exchange(six, 1)

    smem = pl.BlockSpec(memory_space=pltpu.SMEM)
    vmem = pl.BlockSpec(memory_space=pltpu.VMEM)
    anywhere = pl.BlockSpec(memory_space=pl.ANY)
    block = jnp.stack([mine] + arrived)
    weights = around_y(block)
    swapped = []
    for order in ORDER:
        group = jnp.stack([weights[by] for by in order])
        swapped.append(lax.ppermute(group, "core", [(0, 1), (1, 0)]))

    def project(batches, start, dtype):
        count = sum(len(ORDER[batch]) for batch in batches)
        used = [weights[by] for batch in batches for by in ORDER[batch]]
        used += [swapped[batch] for batch in batches]
        return pl.pallas_call(
            functools.partial(project_kernel, batches),
            out_shape=sds((rows, chans), dtype),
            in_specs=[smem] + [anywhere] * (6 + len(used)) + [vmem],
            out_specs=vmem,
            scratch_shapes=[
                pltpu.VMEM((8, rows, chans), BF16),
                pltpu.VMEM((count, 2, 4, 2, WROWS, chans), BF16),
                pltpu.SemaphoreType.DMA((8,)),
                pltpu.SemaphoreType.DMA((count, 8)),
            ],
            cost_estimate=cost(2 * rows * count * chans * chans, 8_000_000),
            name="project",
        )(place, gated, four, two, six, odd, seven, *used, start)

    return project((0, 1, 2), residual, BF16)


def solution(mesh):
    devices = np.asarray(mesh.devices).reshape(8, 2, 4, 2, 8)
    fine = Mesh(devices, ("y", "zh", "x", "core", "tp"))
    ctx = ("y", "zh", "x", "core")
    tp = "tp"
    in_specs = (
        P(ctx, tp),
        P(ctx, None, tp),
        P(None, None, tp),
        P(None, tp),
        P(tp),
        P(ctx, tp),
    )

    return jax.shard_map(
        on_device, mesh=fine, in_specs=in_specs, out_specs=P(ctx, tp), check_vma=False
    )
```
